32 devices in a mesh: grp: 4 (over y, core), ch: 8 (over z, x).
Axes of the slice: x: 2, y: 2, z: 4, core: 2. Of those that a mesh axis runs over, the one named last changes fastest.
Arguments:
- strain: bfloat16 [8, 1024, 4096], P('grp', 'ch'), may hold values from -6 to 6
- valid_mask: int32 [8, 1024], P('grp', 'ch'), may hold values 0 or 1
- pair_list: int32 [8, 6, 2], P('ch'), may hold values from 0 to 7, as said below
- owner_group: int32 [8, 6], P('ch'), may hold values from 0 to 3, as said below
Outputs:
- stacks: float32 [4, 8, 2, 128, 4096], P('grp', 'ch')
The draws below stay inside these ranges and needn't reach their ends.
Inputs may be any that keep to these rules, and one draw needn't show every extreme that they name: `pair_list`: entries are channel block numbers; each ordered pair of blocks appears at most once over all columns. `owner_group`: in each column no group owns more than 2 entries, and some group owns exactly 2.
All inputs are finite; a program needn't handle non-finite values. No bound on the sum of `valid_mask` on one device may be relied on, other than what follows from the above.
Results may differ from the reference program's by a relative error of at most 0.0042.
Values may be sent and summed in bfloat16 or wider, within the bound.
A program may use at most 192 MiB of HBM per device.

```python
import math
import jax
import jax.numpy as jnp
from jax import lax

NFFT = 4096
NB = 1024
SUB = 64
BLK = 128
CAP = 2
GROUPS = 4
COLUMNS = 8
CHANNELS = 1024
WINDOWS = 8
LIST = 6


def draw_pair_list(key, part):
    blocks = CHANNELS // BLK
    pair_codes = jax.random.permutation(key, blocks * blocks)[:COLUMNS * LIST]
    first_block = pair_codes // blocks
    second_block = pair_codes % blocks
    return jnp.stack([first_block, second_block], axis=-1).reshape(COLUMNS, LIST, 2).astype(jnp.int32)


def owner_column(column_key):
    key_slots, key_order = jax.random.split(column_key)
    slot_perm = jax.random.permutation(key_slots, GROUPS * CAP)
    slot_groups = slot_perm // CAP
    head_group = slot_groups[0]
    ordering = jnp.argsort(jnp.where(slot_groups == head_group, 0, 1), stable=True)
    chosen = slot_groups[ordering][:LIST]
    return chosen[jax.random.permutation(key_order, LIST)]


def draw_owner_group(key, part):
    column_keys = jax.random.split(jax.random.fold_in(key, 7), COLUMNS)
    return jax.vmap(owner_column)(column_keys).astype(jnp.int32)


def place_ends(entries, stream_key, low, high):
    spot = [jax.random.randint(jax.random.fold_in(stream_key, axis), (), 0, length) for axis, length in enumerate(entries.shape)]
    longest = entries.shape.index(max(entries.shape))
    next_to = spot[:longest] + [(spot[longest] + 1) % entries.shape[longest]] + spot[longest + 1:]
    return entries.at[tuple(spot)].set(low).at[tuple(next_to)].set(high)


def block_scale(own_key, dims, pieces, low, largest):
    factor_of = 1.0
    for dim, shards_of in pieces:
        steps = jax.random.uniform(jax.random.fold_in(jax.random.fold_in(own_key, 6), dim), (shards_of,), jnp.float32, low / len(pieces), largest / len(pieces))
        factor_of = factor_of * jnp.repeat(jnp.exp(steps), dims[dim] // shards_of).reshape((-1,) + (1,) * (len(dims) - 1 - dim))
    return factor_of


def centred(key, shape, deviation, most, cuts=(), held_as=jnp.bfloat16):
    level = block_scale(key, shape, cuts, -0.22, 0.18) if cuts else 1.0
    drawn = jax.random.normal(key, shape, jnp.float32) * deviation * level
    return jnp.minimum(jnp.maximum(drawn, -most), most).astype(held_as)


def setup_inputs(seed: int = 0) -> dict:
    key_of = jax.random.split(jax.random.key(seed), 5)
    strain = centred(key_of[0], (WINDOWS, CHANNELS, NFFT), 1.0, 6.0, ((0, 4), (1, 8)))
    valid_mask = place_ends((jax.random.randint(key_of[1], (WINDOWS, CHANNELS), 0, 4) < 3).astype(jnp.int32), jax.random.fold_in(key_of[1], 1), 0, 1)
    pair_list = draw_pair_list(jax.random.fold_in(key_of[4], 71), 0)
    owner_group = draw_owner_group(jax.random.fold_in(key_of[4], 71), 0)
    return dict(strain=strain, valid_mask=valid_mask, pair_list=pair_list, owner_group=owner_group)


def forward_table(length, bins):
    samples = jnp.arange(length, dtype=jnp.int32)
    frequency = jnp.arange(1, bins + 1, dtype=jnp.int32)
    angles = jnp.mod(samples[:, None] * frequency[None, :], length).astype(jnp.float32) * (2.0 * math.pi / length)
    hann_taper = 0.5 - 0.5 * jnp.cos(samples.astype(jnp.float32) * (2.0 * math.pi / length))
    return jnp.concatenate([hann_taper[:, None] * jnp.cos(angles), -hann_taper[:, None] * jnp.sin(angles)], axis=1).astype(jnp.bfloat16)

def inverse_table(length, bins):
    frequency = jnp.arange(1, bins + 1, dtype=jnp.int32)
    lag_index = jnp.arange(length, dtype=jnp.int32) - length // 2
    angles = jnp.mod(frequency[:, None] * lag_index[None, :], length).astype(jnp.float32) * (2.0 * math.pi / length)
    return jnp.concatenate([jnp.cos(angles), -jnp.sin(angles)], axis=0)

def whiten_rows(spectrum, valid_mask, bins, band):
    real_part = spectrum[..., :bins]
    imag_part = spectrum[..., bins:]
    power = real_part * real_part + imag_part * imag_part
    band_power = lax.optimization_barrier(jnp.sum(power.reshape(power.shape[:-1] + (bins // band, band)), axis=-1)) / band
    norm_full = jnp.repeat(jnp.sqrt(band_power + 1e-06), band, axis=-1)
    norm_both = jnp.concatenate([norm_full, norm_full], axis=-1)
    return (spectrum / norm_both * valid_mask[..., None].astype(jnp.float32)).astype(jnp.bfloat16)

def cross_block(rows, pair_entry, block, bins):
    first_rows = lax.dynamic_slice_in_dim(rows, (pair_entry[0] * block).astype(jnp.int32), block, 1).astype(jnp.float32)
    second_rows = lax.dynamic_slice_in_dim(rows, (pair_entry[1] * block).astype(jnp.int32), block, 1).astype(jnp.float32)
    first_real = first_rows[..., :bins]
    first_imag = first_rows[..., bins:]
    second_real = second_rows[..., :bins]
    second_imag = second_rows[..., bins:]
    cross_real = lax.optimization_barrier(jnp.sum(first_real * second_real + first_imag * second_imag, axis=0))
    cross_imag = lax.optimization_barrier(jnp.sum(first_real * second_imag - first_imag * second_real, axis=0))
    return jnp.concatenate([cross_real, cross_imag], axis=-1)

def reference(strain, valid_mask, pair_list, owner_group):
    forward = forward_table(NFFT, NB).astype(jnp.float32)
    spectrum = jnp.dot(strain.reshape(-1, NFFT).astype(jnp.float32), forward, precision=lax.Precision.HIGHEST, preferred_element_type=jnp.float32)
    spectrum = spectrum.reshape(WINDOWS, CHANNELS, 2 * NB)
    white = whiten_rows(spectrum, valid_mask, NB, SUB)
    pair_codes = pair_list.reshape(-1, 2)
    cross = lax.map(lambda pair_entry: cross_block(white, pair_entry, BLK, NB), pair_codes)
    cross_flat = cross.reshape(COLUMNS, LIST, BLK * 2 * NB)
    positions = jnp.arange(LIST, dtype=jnp.int32)
    earlier = positions[None, :] < positions[:, None]
    same_owner = owner_group[:, :, None] == owner_group[:, None, :]
    slot_rank = lax.optimization_barrier(jnp.sum((same_owner & earlier[None, :, :]).astype(jnp.int32), axis=2))
    slot_ids = jnp.arange(CAP, dtype=jnp.int32)
    inverse = inverse_table(NFFT, NB)
    scale = 1.0 / math.sqrt(NB * WINDOWS)

    def one_group(group_id):
        picking = ((owner_group[:, None, :] == group_id) & (slot_rank[:, None, :] == slot_ids[None, :, None])).astype(jnp.float32)
        stack = jnp.einsum('csl,clf->csf', picking, cross_flat, precision=lax.Precision.HIGHEST)
        stacked = jnp.dot(stack.reshape(-1, 2 * NB), inverse, precision=lax.Precision.HIGHEST, preferred_element_type=jnp.float32)
        return (stacked * scale).reshape(COLUMNS, CAP, BLK, NFFT)
    return lax.map(one_group, jnp.arange(GROUPS, dtype=jnp.int32))
```

```python
import functools
import math

import jax
import jax.numpy as jnp
import numpy as np
from jax import lax
from jax.experimental import pallas as pl
from jax.experimental.pallas import tpu as pltpu
from jax.sharding import PartitionSpec as P

NFFT = 4096
NB = 1024
SUB = 64
BLK = 128
CAP = 2
LANES = 128
MESH = pl.DeviceIdType.MESH


def row_bins(devices):
    bins = (np.arange(NB, dtype=np.int64) + 1).reshape(devices, 1, NB // devices)
    return np.broadcast_to(bins, (devices, 2, NB // devices)).reshape(-1)


def table_rows(devices, samples, taper):
    angles = np.mod(row_bins(devices)[:, None] * samples[None, :], NFFT) * (2.0 * math.pi / NFFT)
    is_imag = np.broadcast_to(
        np.array([False, True]).reshape(1, 2, 1), (devices, 2, NB // devices)
    ).reshape(-1, 1)
    return (np.where(is_imag, -np.sin(angles), np.cos(angles)) * taper[None, :]).astype(jnp.bfloat16)


@functools.lru_cache(maxsize=None)
def forward_rows(devices):
    samples = np.arange(NFFT, dtype=np.int64)
    taper = 0.5 - 0.5 * np.cos(samples * (2.0 * math.pi / NFFT))
    return table_rows(devices, samples, taper)


@functools.lru_cache(maxsize=None)
def inverse_rows(devices):
    return table_rows(devices, np.arange(NFFT, dtype=np.int64) - NFFT // 2, np.ones(NFFT))


def greet_all(groups, columns, me):
    devices = groups * columns
    barrier = pltpu.get_barrier_semaphore()

    def greet(step, carry):
        to = lax.rem(me + step, devices)
        pl.semaphore_signal(
            barrier,
            inc=1,
            device_id=(lax.div(to, columns), lax.rem(to, columns)),
            device_id_type=MESH,
        )
        return carry

    lax.fori_loop(1, devices, greet, 0)
    pl.semaphore_wait(barrier, devices - 1)


def block_copy(groups, columns, me, step, x_ref, y_ref, send_sem, recv_sem):
    to = lax.rem(me + step, groups * columns)
    return pltpu.make_async_remote_copy(
        src_ref=x_ref.at[to],
        dst_ref=y_ref.at[me],
        send_sem=send_sem.at[step],
        recv_sem=recv_sem.at[step],
        device_id=(lax.div(to, columns), lax.rem(to, columns)),
        device_id_type=MESH,
    )


def list_copy(columns, mine, step, list_ref, lists_ref, send_sem, recv_sem):
    return pltpu.make_async_remote_copy(
        src_ref=list_ref,
        dst_ref=lists_ref.at[mine],
        send_sem=send_sem.at[step],
        recv_sem=recv_sem.at[step],
        device_id=(lax.axis_index("grp"), lax.rem(mine + step, columns)),
        device_id_type=MESH,
    )


def loop(low, high, body):
    def step_body(step, carry):
        body(step)
        return carry

    lax.fori_loop(low, high, step_body, 0)


def exchange_kernel(groups, columns, with_lists, *refs):
    if with_lists:
        x_ref, list_ref, y_ref, lists_ref, own_sem, send_sem, recv_sem, lsend_sem, lrecv_sem = refs
    else:
        x_ref, y_ref, own_sem, send_sem, recv_sem = refs
    devices = groups * columns
    mine = lax.axis_index("ch")
    me = lax.axis_index("grp") * columns + mine
    greet_all(groups, columns, me)

    def copy_of(step):
        return block_copy(groups, columns, me, step, x_ref, y_ref, send_sem, recv_sem)

    def list_of(step):
        return list_copy(columns, mine, step, list_ref, lists_ref, lsend_sem, lrecv_sem)

    if with_lists:
        loop(1, columns, lambda step: list_of(step).start())
    loop(1, devices, lambda step: copy_of(step).start())
    own = pltpu.make_async_copy(x_ref.at[me], y_ref.at[me], own_sem.at[0])
    own.start()
    own.wait()
    if with_lists:
        own_list = pltpu.make_async_copy(list_ref, lists_ref.at[mine], own_sem.at[1])
        own_list.start()
        own_list.wait()
        loop(1, columns, lambda step: list_of(step).wait())
    loop(1, devices, lambda step: copy_of(step).wait())


def exchange(x, groups, columns, collective_id, own_list=None):
    devices = groups * columns
    with_lists = own_list is not None
    vmem = pl.BlockSpec(memory_space=pltpu.VMEM)
    out_shape = [jax.ShapeDtypeStruct(x.shape, x.dtype)]
    scratch = [
        pltpu.SemaphoreType.DMA((2,)),
        pltpu.SemaphoreType.DMA((devices,)),
        pltpu.SemaphoreType.DMA((devices,)),
    ]
    operands = [x]
    if with_lists:
        operands.append(own_list)
        out_shape.append(jax.ShapeDtypeStruct((columns,) + own_list.shape, own_list.dtype))
        scratch += [pltpu.SemaphoreType.DMA((columns,)), pltpu.SemaphoreType.DMA((columns,))]
    out = pl.pallas_call(
        functools.partial(exchange_kernel, groups, columns, with_lists),
        out_shape=out_shape,
        in_specs=[vmem] * len(operands),
        out_specs=[vmem] * len(out_shape),
        scratch_shapes=scratch,
        compiler_params=pltpu.CompilerParams(collective_id=collective_id, has_side_effects=True),
    )(*operands)
    return out if with_lists else out[0]


def cross_kernel(groups, columns, entries, scale, lists_ref, rows_ref, out_ref):
    half = rows_ref.shape[1] // 2
    windows = rows_ref.shape[2] // BLK
    out_ref[...] = jnp.zeros_like(out_ref)

    def column_body(column):
        for entry in range(entries):
            first = lists_ref[column, 2 * entry]
            second = lists_ref[column, 2 * entry + 1]
            owner = lists_ref[column, 2 * entries + entry]
            rank = jnp.int32(0)
            for before in range(entry):
                rank += (lists_ref[column, 2 * entries + before] == owner).astype(jnp.int32)
            real = jnp.zeros((half, BLK), jnp.float32)
            imag = jnp.zeros((half, BLK), jnp.float32)
            for group in range(groups):
                a = rows_ref[group * columns + first].astype(jnp.float32)
                b = rows_ref[group * columns + second].astype(jnp.float32)
                for window in range(windows):
                    lanes = slice(window * BLK, (window + 1) * BLK)
                    a_real, a_imag = a[:half, lanes], a[half:, lanes]
                    b_real, b_imag = b[:half, lanes], b[half:, lanes]
                    real += a_real * b_real + a_imag * b_imag
                    imag += a_real * b_imag - a_imag * b_real
            both = jnp.concatenate([real, imag], axis=0) * scale
            out_ref[owner * columns + column, rank] = both.astype(out_ref.dtype)

    loop(0, columns, column_body)


def local(strain, valid_mask, pair_list, owner_group):
    windows, channels = valid_mask.shape
    groups = lax.axis_size("grp")
    columns = lax.axis_size("ch")
    devices = groups * columns
    entries = owner_group.shape[1]
    rows = 2 * NB // devices

    forward = jnp.asarray(forward_rows(devices))
    spectrum = lax.dot_general(
        forward,
        strain.reshape(windows * channels, NFFT),
        (((1,), (1,)), ((), ())),
        preferred_element_type=jnp.float32,
    ).reshape(devices, 2, rows // 2, windows * channels)
    power = jnp.sum(spectrum * spectrum, axis=1)
    band_power = jnp.sum(power.reshape(NB // SUB, SUB, -1), axis=1) / SUB
    gain = valid_mask.reshape(1, -1).astype(jnp.float32) / jnp.sqrt(band_power + 1e-06)
    gain = jnp.repeat(gain, SUB, axis=0).reshape(devices, 1, rows // 2, windows * channels)
    white = (spectrum * gain).astype(jnp.bfloat16).reshape(devices, rows, windows * channels)

    flat = jnp.concatenate([pair_list.reshape(-1), owner_group.reshape(-1)])
    own_list = jnp.broadcast_to(jnp.pad(flat, (0, LANES - flat.shape[0])), (8, LANES))
    gathered, lists = exchange(white, groups, columns, 0, own_list)

    scale = 1.0 / math.sqrt(NB * windows * groups)
    vmem = pl.BlockSpec(memory_space=pltpu.VMEM)
    slots = pl.pallas_call(
        functools.partial(cross_kernel, groups, columns, entries, scale),
        out_shape=jax.ShapeDtypeStruct((devices, CAP, rows, BLK), jnp.bfloat16),
        in_specs=[pl.BlockSpec(memory_space=pltpu.SMEM), vmem],
        out_specs=vmem,
    )(lists[:, 0, : 3 * entries], gathered)

    stack = exchange(slots, groups, columns, 1)
    stack = stack.transpose(1, 0, 2, 3).reshape(CAP, 2 * NB, BLK)
    stacked = jnp.einsum(
        "skr,kt->srt",
        stack,
        jnp.asarray(inverse_rows(devices)),
        preferred_element_type=jnp.float32,
    )
    return stacked.reshape(1, 1, CAP, BLK, NFFT)


def solution(mesh):
    placed = (P("grp", "ch", None), P("grp", "ch"), P("ch", None, None), P("ch", None))
    return jax.shard_map(
        local,
        mesh=mesh,
        in_specs=placed,
        out_specs=P("grp", "ch", None, None, None),
        check_vma=False,
    )
```

```python
import functools
import math

import jax
import jax.numpy as jnp
import numpy as np
from jax import lax
from jax.experimental import pallas as pl
from jax.experimental.pallas import tpu as pltpu
from jax.sharding import PartitionSpec as P

NFFT = 4096
NB = 1024
SUB = 64
BLK = 128
CAP = 2
LANES = 128
PHASES = 2
MESH = pl.DeviceIdType.MESH


def phases_of(devices):
    return max(1, min(PHASES, NB // devices // 8))


def table_rows(devices, samples, taper):
    phases = phases_of(devices)
    bins = (np.arange(NB, dtype=np.int64) + 1).reshape(phases, devices, 1, -1, 1)
    angles = np.mod(bins * samples, NFFT) * (2.0 * math.pi / NFFT)
    rows = np.concatenate([np.cos(angles), -np.sin(angles)], axis=2) * taper
    return rows.reshape(2 * NB, NFFT).astype(jnp.bfloat16)


@functools.lru_cache(maxsize=None)
def forward_rows(devices):
    samples = np.arange(NFFT, dtype=np.int64)
    taper = 0.5 - 0.5 * np.cos(samples * (2.0 * math.pi / NFFT))
    return table_rows(devices, samples, taper)


@functools.lru_cache(maxsize=None)
def inverse_rows(devices):
    return table_rows(devices, np.arange(NFFT, dtype=np.int64) - NFFT // 2, np.ones(NFFT))


def loop(low, high, body):
    def step_body(step, carry):
        body(step)
        return carry

    lax.fori_loop(low, high, step_body, 0)


def slot_row(groups, entries, pairs_ref, owners_ref):
    lane = lax.broadcasted_iota(jnp.int32, (8, LANES), 1)
    row = jnp.zeros((8, LANES), jnp.int32)
    for entry in range(entries):
        owner = owners_ref[0, entry]
        rank = jnp.int32(0)
        for before in range(entry):
            rank += (owners_ref[0, before] == owner).astype(jnp.int32)
        base = 3 * (owner * CAP + rank)
        row = jnp.where(lane == base, pairs_ref[0, 0, entry], row)
        row = jnp.where(lane == base + 1, pairs_ref[0, 1, entry], row)
        row = jnp.where(lane == base + 2, 1, row)
    return row


def correlate_kernel(
    groups, columns, phases, entries, windows, scale,
    pairs_ref, owners_ref, mask_ref, strain_ref, table_ref,
    stack_ref,
    table_buf, white_buf, list_buf, lists_buf, lists_smem, *rest,
):
    rows_bufs, slot_bufs = rest[:phases], rest[phases : 2 * phases]
    table_sem, own_sem, lsend_sem, lrecv_sem, wsend_sem, wrecv_sem, ssend_sem, srecv_sem = rest[
        2 * phases :
    ]
    devices = groups * columns
    my_group = lax.axis_index("grp")
    mine = lax.axis_index("ch")
    me = my_group * columns + mine
    tiles = phases * groups
    rows = white_buf.shape[2]
    half = rows // 2

    def tile_group(index):
        return lax.rem(index + my_group, groups)

    def tile_copy(index):
        place = lax.div(index, groups) * groups + tile_group(index)
        return pltpu.make_async_copy(
            table_ref.at[place], table_buf.at[index], table_sem.at[index]
        )

    loop(0, tiles, lambda index: tile_copy(index).start())

    barrier = pltpu.get_barrier_semaphore()

    def greet(step):
        to = lax.rem(me + step, devices)
        pl.semaphore_signal(
            barrier,
            inc=1,
            device_id=(lax.div(to, columns), lax.rem(to, columns)),
            device_id_type=MESH,
        )

    loop(1, devices, greet)
    list_buf[...] = slot_row(groups, entries, pairs_ref, owners_ref)

    def compute_tile(index):
        tile_copy(index).wait()
        spectrum = lax.dot_general(
            table_buf[index],
            strain_ref[...],
            (((1,), (1,)), ((), ())),
            preferred_element_type=jnp.float32,
        )
        lanes = spectrum.shape[1]
        parts = spectrum.reshape(columns, 2, half, lanes)
        power = parts[:, 0] * parts[:, 0] + parts[:, 1] * parts[:, 1]
        bands = columns * half // SUB
        band_power = jnp.sum(power.reshape(bands, SUB, lanes), axis=1, keepdims=True) / SUB
        usable = jnp.concatenate([mask_ref[w : w + 1, :] for w in range(windows)], axis=1)
        gain = usable.astype(jnp.float32).reshape(1, 1, lanes) / jnp.sqrt(band_power + 1e-06)
        gain = jnp.broadcast_to(gain, (bands, SUB, lanes)).reshape(columns, 1, half, lanes)
        white_buf[index] = (parts * gain).reshape(columns, rows, lanes).astype(jnp.bfloat16)

    def white_copy(phase, index, column):
        to_group = tile_group(index)
        to = to_group * columns + column
        return pltpu.make_async_remote_copy(
            src_ref=white_buf.at[index, column],
            dst_ref=rows_bufs[phase].at[me],
            send_sem=wsend_sem.at[phase, to],
            recv_sem=wrecv_sem.at[phase, me],
            device_id=(to_group, column),
            device_id_type=MESH,
        )

    def white_own(phase, index):
        return pltpu.make_async_copy(
            white_buf.at[index, mine], rows_bufs[phase].at[me], wrecv_sem.at[phase, me]
        )

    def send_tile(phase, index):
        def send(step):
            column = lax.rem(mine + step, columns)
            away = (tile_group(index) != my_group) | (column != mine)

            @pl.when(away)
            def _():
                white_copy(phase, index, column).start()

            @pl.when(jnp.logical_not(away))
            def _():
                white_own(phase, index).start()

        loop(0, columns, send)

    def list_copy(step):
        return pltpu.make_async_remote_copy(
            src_ref=list_buf,
            dst_ref=lists_buf.at[mine],
            send_sem=lsend_sem.at[step],
            recv_sem=lrecv_sem.at[step],
            device_id=(my_group, lax.rem(mine + step, columns)),
            device_id_type=MESH,
        )

    compute_tile(0)
    pl.semaphore_wait(barrier, devices - 1)
    loop(1, columns, lambda step: list_copy(step).start())
    own_list = pltpu.make_async_copy(list_buf, lists_buf.at[mine], own_sem.at[0])
    own_list.start()
    for phase in range(phases):

        def compute_and_send(index, phase=phase):
            compute_tile(index)
            send_tile(phase, index - 1)

        loop(phase * groups + 1, (phase + 1) * groups, compute_and_send)
        if phase + 1 < phases:
            compute_tile((phase + 1) * groups)
        send_tile(phase, (phase + 1) * groups - 1)

    own_list.wait()
    loop(1, columns, lambda step: list_copy(step).wait())
    to_smem = pltpu.make_async_copy(lists_buf, lists_smem, own_sem.at[1])
    to_smem.start()
    to_smem.wait()

    def slot_copy(phase, group, column):
        return pltpu.make_async_remote_copy(
            src_ref=slot_bufs[phase].at[group, column],
            dst_ref=stack_ref.at[:, phase, me],
            send_sem=ssend_sem.at[phase, group * columns + column],
            recv_sem=srecv_sem.at[phase, me],
            device_id=(group, column),
            device_id_type=MESH,
        )

    def slot_own(phase):
        return pltpu.make_async_copy(
            slot_bufs[phase].at[my_group, mine], stack_ref.at[:, phase, me], srecv_sem.at[phase, me]
        )

    def cross_column(phase, column):
        rows_ref = rows_bufs[phase]
        for owner in range(groups):
            for rank in range(CAP):
                base = 3 * (owner * CAP + rank)
                first = lists_smem[column, 0, base]
                second = lists_smem[column, 0, base + 1]
                factor = lists_smem[column, 0, base + 2].astype(jnp.float32) * scale
                real = jnp.zeros((half, BLK), jnp.float32)
                imag = jnp.zeros((half, BLK), jnp.float32)
                for group in range(groups):
                    a = rows_ref[group * columns + first].astype(jnp.float32)
                    b = rows_ref[group * columns + second].astype(jnp.float32)
                    for window in range(windows):
                        lanes = slice(window * BLK, (window + 1) * BLK)
                        a_real, a_imag = a[:half, lanes], a[half:, lanes]
                        b_real, b_imag = b[:half, lanes], b[half:, lanes]
                        real += a_real * b_real + a_imag * b_imag
                        imag += a_real * b_imag - a_imag * b_real
                both = jnp.concatenate([real, imag], axis=0) * factor
                slot_bufs[phase][owner, column, rank] = both.astype(jnp.bfloat16)

    def send_column(phase, column):
        def send(step):
            group = lax.rem(my_group + step, groups)
            away = (group != my_group) | (column != mine)

            @pl.when(away)
            def _():
                slot_copy(phase, group, column).start()

            @pl.when(jnp.logical_not(away))
            def _():
                slot_own(phase).start()

        loop(0, groups, send)

    def wait_from(phase, sem, part):
        def wait(source):
            @pl.when(source != me)
            def _():
                pltpu.make_async_remote_copy(
                    src_ref=part(source),
                    dst_ref=part(source),
                    send_sem=sem.at[phase, source],
                    recv_sem=sem.at[phase, source],
                    device_id=(lax.div(source, columns), lax.rem(source, columns)),
                    device_id_type=MESH,
                ).wait_recv()

        loop(0, devices, wait)

    for phase in range(phases):
        white_own(phase, phase * groups).wait()
        wait_from(phase, wrecv_sem, lambda source: rows_bufs[phase].at[source])

        cross_column(phase, mine)

        def cross_and_send(step, phase=phase):
            cross_column(phase, lax.rem(mine + step, columns))
            send_column(phase, lax.rem(mine + step - 1, columns))

        loop(1, columns, cross_and_send)
        send_column(phase, lax.rem(mine + columns - 1, columns))

    for phase in range(phases):
        slot_own(phase).wait()
        wait_from(phase, srecv_sem, lambda source: stack_ref.at[:, phase, source])

        def wait_sends(to, phase=phase):
            group, column = lax.div(to, columns), lax.rem(to, columns)

            @pl.when(to != me)
            def _():
                index = phase * groups + lax.rem(group - my_group + groups, groups)
                white_copy(phase, index, column).wait_send()
                slot_copy(phase, group, column).wait_send()

        loop(0, devices, wait_sends)


def local(strain, valid_mask, pair_list, owner_group):
    windows, channels = valid_mask.shape
    groups = lax.axis_size("grp")
    columns = lax.axis_size("ch")
    devices = groups * columns
    entries = owner_group.shape[1]
    phases = phases_of(devices)
    rows = 2 * NB // devices // phases
    lanes = windows * channels
    tiles = phases * groups
    scale = 1.0 / math.sqrt(NB * windows * groups)

    vmem = pl.BlockSpec(memory_space=pltpu.VMEM)
    smem = pl.BlockSpec(memory_space=pltpu.SMEM)
    dma = pltpu.SemaphoreType.DMA
    stack = pl.pallas_call(
        functools.partial(correlate_kernel, groups, columns, phases, entries, windows, scale),
        out_shape=jax.ShapeDtypeStruct((CAP, phases, devices, rows, BLK), jnp.bfloat16),
        in_specs=[smem, smem, vmem, vmem, pl.BlockSpec(memory_space=pl.ANY)],
        out_specs=vmem,
        scratch_shapes=[
            pltpu.VMEM((tiles, columns * rows, NFFT), jnp.bfloat16),
            pltpu.VMEM((tiles, columns, rows, lanes), jnp.bfloat16),
            pltpu.VMEM((8, LANES), jnp.int32),
            pltpu.VMEM((columns, 8, LANES), jnp.int32),
            pltpu.SMEM((columns, 8, LANES), jnp.int32),
        ]
        + [pltpu.VMEM((devices, rows, lanes), jnp.bfloat16) for _ in range(phases)]
        + [pltpu.VMEM((groups, columns, CAP, rows, BLK), jnp.bfloat16) for _ in range(phases)]
        + [dma((tiles,)), dma((2,)), dma((columns,)), dma((columns,))]
        + [dma((phases, devices)) for _ in range(4)],
        compiler_params=pltpu.CompilerParams(
            collective_id=0, has_side_effects=True, vmem_limit_bytes=48 * 1024 * 1024
        ),
    )(
        pair_list.transpose(0, 2, 1),
        owner_group,
        valid_mask,
        strain.reshape(lanes, NFFT),
        jnp.asarray(forward_rows(devices)).reshape(tiles, columns * rows, NFFT),
    )
    stacked = jnp.einsum(
        "skr,kt->srt",
        stack.reshape(CAP, 2 * NB, BLK),
        jnp.asarray(inverse_rows(devices)),
        preferred_element_type=jnp.float32,
    )
    return stacked.reshape(1, 1, CAP, BLK, NFFT)


def solution(mesh):
    placed = (P("grp", "ch", None), P("grp", "ch"), P("ch", None, None), P("ch", None))
    return jax.shard_map(
        local,
        mesh=mesh,
        in_specs=placed,
        out_specs=P("grp", "ch", None, None, None),
        check_vma=False,
    )
```

```python
import functools
import math

import jax
import jax.numpy as jnp
import numpy as np
from jax import lax
from jax.experimental import pallas as pl
from jax.experimental.pallas import tpu as pltpu
from jax.sharding import PartitionSpec as P

NFFT = 4096
NB = 1024
SUB = 64
BLK = 128
CAP = 2
LANES = 128
PHASES = 2
LAGS = 512
MESH = pl.DeviceIdType.MESH


def phases_of(devices):
    return max(1, min(PHASES, NB // devices // 8))


def table_rows(devices, samples, taper):
    phases = phases_of(devices)
    bins = (np.arange(NB, dtype=np.int64) + 1).reshape(phases, devices, 1, -1, 1)
    angles = np.mod(bins * samples, NFFT) * (2.0 * math.pi / NFFT)
    rows = np.concatenate([np.cos(angles), -np.sin(angles)], axis=2) * taper
    return rows.reshape(2 * NB, NFFT).astype(jnp.bfloat16)


@functools.lru_cache(maxsize=None)
def forward_rows(devices):
    samples = np.arange(NFFT, dtype=np.int64)
    taper = 0.5 - 0.5 * np.cos(samples * (2.0 * math.pi / NFFT))
    return table_rows(devices, samples, taper)


@functools.lru_cache(maxsize=None)
def inverse_rows(devices):
    return table_rows(devices, np.arange(NFFT, dtype=np.int64) - NFFT // 2, np.ones(NFFT))


def loop(low, high, body):
    def step_body(step, carry):
        body(step)
        return carry

    lax.fori_loop(low, high, step_body, 0)


def slot_row(groups, entries, pairs_ref, owners_ref):
    lane = lax.broadcasted_iota(jnp.int32, (8, LANES), 1)
    row = jnp.zeros((8, LANES), jnp.int32)
    for entry in range(entries):
        owner = owners_ref[0, entry]
        rank = jnp.int32(0)
        for before in range(entry):
            rank += (owners_ref[0, before] == owner).astype(jnp.int32)
        base = 3 * (owner * CAP + rank)
        row = jnp.where(lane == base, pairs_ref[0, 0, entry], row)
        row = jnp.where(lane == base + 1, pairs_ref[0, 1, entry], row)
        row = jnp.where(lane == base + 2, 1, row)
    return row


def correlate_kernel(
    groups, columns, phases, entries, windows, scale,
    pairs_hbm, owners_hbm, mask_hbm, strain_hbm, table_ref, inverse_ref, *rest,
):
    outs = 2 if phases > 1 else 1
    last_stack, total_hbm = rest[0], rest[outs - 1]
    pairs_ref, owners_ref, mask_ref, strain_ref, inverse_buf, left_buf = rest[outs : outs + 6]
    table_buf, white_buf, list_buf, lists_buf, lists_smem = rest[outs + 6 : outs + 11]
    total_ref, total_sem = rest[outs + 11 : outs + 13]
    rest = rest[outs + 13 :]
    rows_bufs, slot_bufs = rest[:phases], rest[phases : 2 * phases]
    stack_bufs = list(rest[2 * phases : 3 * phases - 1]) + [last_stack]
    in_sem, inverse_sem = rest[3 * phases - 1 : 3 * phases + 1]
    table_sem, own_sem, lsend_sem, lrecv_sem, wsend_sem, wrecv_sem, ssend_sem, srecv_sem = rest[
        3 * phases + 1 :
    ]
    devices = groups * columns
    my_group = lax.axis_index("grp")
    mine = lax.axis_index("ch")
    me = my_group * columns + mine
    tiles = phases * groups
    rows = white_buf.shape[2]
    half = rows // 2

    def tile_group(index):
        return lax.rem(index + my_group, groups)

    def tile_copy(index):
        place = lax.div(index, groups) * groups + tile_group(index)
        return pltpu.make_async_copy(
            table_ref.at[place], table_buf.at[index], table_sem.at[index]
        )

    inputs = [
        pltpu.make_async_copy(source, target, in_sem.at[place])
        for place, (source, target) in enumerate(
            [
                (pairs_hbm, pairs_ref),
                (owners_hbm, owners_ref),
                (mask_hbm, mask_ref),
                (strain_hbm, strain_ref),
            ]
        )
    ]
    for copy in inputs:
        copy.start()
    loop(0, tiles, lambda index: tile_copy(index).start())

    def inverse_copy(phase):
        return pltpu.make_async_copy(
            inverse_ref.at[phase], inverse_buf.at[phase], inverse_sem.at[phase]
        )

    for phase in range(phases - 1):
        inverse_copy(phase).start()

    barrier = pltpu.get_barrier_semaphore()

    def greet(step):
        to = lax.rem(me + step, devices)
        pl.semaphore_signal(
            barrier,
            inc=1,
            device_id=(lax.div(to, columns), lax.rem(to, columns)),
            device_id_type=MESH,
        )

    loop(1, devices, greet)
    for copy in inputs:
        copy.wait()
    list_buf[...] = slot_row(groups, entries, pairs_ref, owners_ref)

    def compute_tile(index):
        tile_copy(index).wait()
        spectrum = lax.dot_general(
            table_buf[index],
            strain_ref[...],
            (((1,), (1,)), ((), ())),
            preferred_element_type=jnp.float32,
        )
        lanes = spectrum.shape[1]
        parts = spectrum.reshape(columns, 2, half, lanes)
        power = parts[:, 0] * parts[:, 0] + parts[:, 1] * parts[:, 1]
        bands = columns * half // SUB
        band_power = jnp.sum(power.reshape(bands, SUB, lanes), axis=1, keepdims=True) / SUB
        usable = jnp.concatenate([mask_ref[w : w + 1, :] for w in range(windows)], axis=1)
        gain = usable.astype(jnp.float32).reshape(1, 1, lanes) / jnp.sqrt(band_power + 1e-06)
        gain = jnp.broadcast_to(gain, (bands, SUB, lanes)).reshape(columns, 1, half, lanes)
        white_buf[index] = (parts * gain).reshape(columns, rows, lanes).astype(jnp.bfloat16)

    def white_copy(phase, index, column):
        to_group = tile_group(index)
        to = to_group * columns + column
        return pltpu.make_async_remote_copy(
            src_ref=white_buf.at[index, column],
            dst_ref=rows_bufs[phase].at[me],
            send_sem=wsend_sem.at[phase, to],
            recv_sem=wrecv_sem.at[phase, me],
            device_id=(to_group, column),
            device_id_type=MESH,
        )

    def white_own(phase, index):
        return pltpu.make_async_copy(
            white_buf.at[index, mine], rows_bufs[phase].at[me], wrecv_sem.at[phase, me]
        )

    def send_tile(phase, index):
        def send(step):
            column = lax.rem(mine + step, columns)
            away = (tile_group(index) != my_group) | (column != mine)

            @pl.when(away)
            def _():
                white_copy(phase, index, column).start()

            @pl.when(jnp.logical_not(away))
            def _():
                white_own(phase, index).start()

        loop(0, columns, send)

    def list_copy(step):
        return pltpu.make_async_remote_copy(
            src_ref=list_buf,
            dst_ref=lists_buf.at[mine],
            send_sem=lsend_sem.at[step],
            recv_sem=lrecv_sem.at[step],
            device_id=(my_group, lax.rem(mine + step, columns)),
            device_id_type=MESH,
        )

    compute_tile(0)
    pl.semaphore_wait(barrier, devices - 1)
    loop(1, columns, lambda step: list_copy(step).start())
    own_list = pltpu.make_async_copy(list_buf, lists_buf.at[mine], own_sem.at[0])
    own_list.start()
    for phase in range(phases):

        def compute_and_send(index, phase=phase):
            compute_tile(index)
            send_tile(phase, index - 1)

        loop(phase * groups + 1, (phase + 1) * groups, compute_and_send)
        if phase + 1 < phases:
            compute_tile((phase + 1) * groups)
        send_tile(phase, (phase + 1) * groups - 1)

    own_list.wait()
    loop(1, columns, lambda step: list_copy(step).wait())
    to_smem = pltpu.make_async_copy(lists_buf, lists_smem, own_sem.at[1])
    to_smem.start()
    to_smem.wait()

    def slot_copy(phase, group, column):
        return pltpu.make_async_remote_copy(
            src_ref=slot_bufs[phase].at[group, column],
            dst_ref=stack_bufs[phase].at[:, me],
            send_sem=ssend_sem.at[phase, group * columns + column],
            recv_sem=srecv_sem.at[phase, me],
            device_id=(group, column),
            device_id_type=MESH,
        )

    def slot_own(phase):
        return pltpu.make_async_copy(
            slot_bufs[phase].at[my_group, mine], stack_bufs[phase].at[:, me], srecv_sem.at[phase, me]
        )

    def cross_column(phase, column):
        rows_ref = rows_bufs[phase]
        for owner in range(groups):
            for rank in range(CAP):
                base = 3 * (owner * CAP + rank)
                first = lists_smem[column, 0, base]
                second = lists_smem[column, 0, base + 1]
                factor = lists_smem[column, 0, base + 2].astype(jnp.float32) * scale
                real = jnp.zeros((half, BLK), jnp.float32)
                imag = jnp.zeros((half, BLK), jnp.float32)
                for group in range(groups):
                    a = rows_ref[group * columns + first].astype(jnp.float32)
                    b = rows_ref[group * columns + second].astype(jnp.float32)
                    for window in range(windows):
                        lanes = slice(window * BLK, (window + 1) * BLK)
                        a_real, a_imag = a[:half, lanes], a[half:, lanes]
                        b_real, b_imag = b[:half, lanes], b[half:, lanes]
                        real += a_real * b_real + a_imag * b_imag
                        imag += a_real * b_imag - a_imag * b_real
                both = jnp.concatenate([real, imag], axis=0) * factor
                slot_bufs[phase][owner, column, rank] = both.astype(jnp.bfloat16)

    def send_column(phase, column):
        def send(step):
            group = lax.rem(my_group + step, groups)
            away = (group != my_group) | (column != mine)

            @pl.when(away)
            def _():
                slot_copy(phase, group, column).start()

            @pl.when(jnp.logical_not(away))
            def _():
                slot_own(phase).start()

        loop(0, groups, send)

    def wait_from(phase, sem, part):
        def wait(source):
            @pl.when(source != me)
            def _():
                pltpu.make_async_remote_copy(
                    src_ref=part(source),
                    dst_ref=part(source),
                    send_sem=sem.at[phase, source],
                    recv_sem=sem.at[phase, source],
                    device_id=(lax.div(source, columns), lax.rem(source, columns)),
                    device_id_type=MESH,
                ).wait_recv()

        loop(0, devices, wait)

    for phase in range(phases):
        white_own(phase, phase * groups).wait()
        wait_from(phase, wrecv_sem, lambda source: rows_bufs[phase].at[source])

        cross_column(phase, mine)

        def cross_and_send(step, phase=phase):
            cross_column(phase, lax.rem(mine + step, columns))
            send_column(phase, lax.rem(mine + step - 1, columns))

        loop(1, columns, cross_and_send)
        send_column(phase, lax.rem(mine + columns - 1, columns))

    for phase in range(phases):
        slot_own(phase).wait()
        wait_from(phase, srecv_sem, lambda source: stack_bufs[phase].at[:, source])
        if phase < phases - 1:
            inverse_copy(phase).wait()
            depth = devices * rows
            for rank in range(CAP):
                block = stack_bufs[phase][rank].reshape(depth, BLK).astype(jnp.float32)
                left_buf[rank * BLK : (rank + 1) * BLK, :] = block.T.astype(jnp.bfloat16)

            def inverse_tile(tile, phase=phase):
                at = pl.ds(pl.multiple_of(tile * LAGS, LAGS), LAGS)
                part = jnp.dot(
                    left_buf[...], inverse_buf[phase, :, at], preferred_element_type=jnp.float32
                )
                total_ref[:, at] = part if phase == 0 else total_ref[:, at] + part

            loop(0, NFFT // LAGS, inverse_tile)
        if phase == phases - 2:
            total_copy = pltpu.make_async_copy(total_ref, total_hbm, total_sem.at[0])
            total_copy.start()


        def wait_sends(to, phase=phase):
            group, column = lax.div(to, columns), lax.rem(to, columns)

            @pl.when(to != me)
            def _():
                index = phase * groups + lax.rem(group - my_group + groups, groups)
                white_copy(phase, index, column).wait_send()
                slot_copy(phase, group, column).wait_send()

        loop(0, devices, wait_sends)
    if phases > 1:
        total_copy.wait()


def local(strain, valid_mask, pair_list, owner_group):
    windows, channels = valid_mask.shape
    groups = lax.axis_size("grp")
    columns = lax.axis_size("ch")
    devices = groups * columns
    entries = owner_group.shape[1]
    phases = phases_of(devices)
    rows = 2 * NB // devices // phases
    lanes = windows * channels
    tiles = phases * groups
    scale = 1.0 / math.sqrt(NB * windows * groups)

    vmem = pl.BlockSpec(memory_space=pltpu.VMEM)
    dma = pltpu.SemaphoreType.DMA
    anywhere = pl.BlockSpec(memory_space=pltpu.HBM)
    stack_shape = (CAP, devices, rows, BLK)
    depth = devices * rows
    outs = [jax.ShapeDtypeStruct(stack_shape, jnp.bfloat16)]
    if phases > 1:
        outs.append(jax.ShapeDtypeStruct((CAP * BLK, NFFT), jnp.float32))
    inverse = inverse_rows(devices).reshape(phases, depth, NFFT)
    stack, *total = pl.pallas_call(
        functools.partial(correlate_kernel, groups, columns, phases, entries, windows, scale),
        out_shape=outs,
        in_specs=[anywhere] * 6,
        out_specs=[vmem, anywhere][: len(outs)],
        scratch_shapes=[
            pltpu.SMEM((1, 2, entries), jnp.int32),
            pltpu.SMEM((1, entries), jnp.int32),
            pltpu.VMEM((windows, channels), jnp.int32),
            pltpu.VMEM((lanes, NFFT), jnp.bfloat16),
            pltpu.VMEM((max(1, phases - 1), depth if phases > 1 else 16, NFFT), jnp.bfloat16),
            pltpu.VMEM((CAP * BLK, depth), jnp.bfloat16),
            pltpu.VMEM((tiles, columns * rows, NFFT), jnp.bfloat16),
            pltpu.VMEM((tiles, columns, rows, lanes), jnp.bfloat16),
            pltpu.VMEM((8, LANES), jnp.int32),
            pltpu.VMEM((columns, 8, LANES), jnp.int32),
            pltpu.SMEM((columns, 8, LANES), jnp.int32),
            pltpu.VMEM((CAP * BLK, NFFT if phases > 1 else LANES), jnp.float32),
            dma((1,)),
        ]
        + [pltpu.VMEM((devices, rows, lanes), jnp.bfloat16) for _ in range(phases)]
        + [pltpu.VMEM((groups, columns, CAP, rows, BLK), jnp.bfloat16) for _ in range(phases)]
        + [pltpu.VMEM(stack_shape, jnp.bfloat16) for _ in range(phases - 1)]
        + [dma((4,)), dma((phases,))]
        + [dma((tiles,)), dma((2,)), dma((columns,)), dma((columns,))]
        + [dma((phases, devices)) for _ in range(4)],
        compiler_params=pltpu.CompilerParams(
            collective_id=0, has_side_effects=True, vmem_limit_bytes=52 * 1024 * 1024
        ),
    )(
        pair_list.transpose(0, 2, 1),
        owner_group,
        valid_mask,
        strain.reshape(lanes, NFFT),
        jnp.asarray(forward_rows(devices)).reshape(tiles, columns * rows, NFFT),
        jnp.asarray(inverse[: max(1, phases - 1)]),
    )
    stacked = jnp.einsum(
        "skr,kt->srt",
        stack.reshape(CAP, depth, BLK),
        jnp.asarray(inverse[phases - 1]),
        preferred_element_type=jnp.float32,
    )
    if phases > 1:
        stacked = stacked + total[0].reshape(CAP, BLK, NFFT)
    return stacked.reshape(1, 1, CAP, BLK, NFFT)


def solution(mesh):
    placed = (P("grp", "ch", None), P("grp", "ch"), P("ch", None, None), P("ch", None))
    return jax.shard_map(
        local,
        mesh=mesh,
        in_specs=placed,
        out_specs=P("grp", "ch", None, None, None),
        check_vma=False,
    )
```

```python
import functools
import math

import jax
import jax.numpy as jnp
import numpy as np
from jax import lax
from jax.experimental import pallas as pl
from jax.experimental.pallas import tpu as pltpu
from jax.sharding import PartitionSpec as P

NFFT = 4096
NB = 1024
SUB = 64
BLK = 128
CAP = 2
LANES = 128
PHASES = 4
LAGS = 512
MESH = pl.DeviceIdType.MESH


def phases_of(devices):
    return max(1, min(PHASES, NB // devices // 8))


def table_rows(devices, samples, taper):
    phases = phases_of(devices)
    bins = (np.arange(NB, dtype=np.int64) + 1).reshape(phases, devices, 1, -1, 1)
    angles = np.mod(bins * samples, NFFT) * (2.0 * math.pi / NFFT)
    rows = np.concatenate([np.cos(angles), -np.sin(angles)], axis=2) * taper
    return rows.reshape(2 * NB, NFFT).astype(jnp.bfloat16)


@functools.lru_cache(maxsize=None)
def forward_rows(devices):
    samples = np.arange(NFFT, dtype=np.int64)
    taper = 0.5 - 0.5 * np.cos(samples * (2.0 * math.pi / NFFT))
    return table_rows(devices, samples, taper)


@functools.lru_cache(maxsize=None)
def inverse_rows(devices):
    return table_rows(devices, np.arange(NFFT, dtype=np.int64) - NFFT // 2, np.ones(NFFT))


def loop(low, high, body):
    def step_body(step, carry):
        body(step)
        return carry

    lax.fori_loop(low, high, step_body, 0)


def slot_row(groups, entries, pairs_ref, owners_ref):
    lane = lax.broadcasted_iota(jnp.int32, (8, LANES), 1)
    row = jnp.zeros((8, LANES), jnp.int32)
    for entry in range(entries):
        owner = owners_ref[0, entry]
        rank = jnp.int32(0)
        for before in range(entry):
            rank += (owners_ref[0, before] == owner).astype(jnp.int32)
        base = 3 * (owner * CAP + rank)
        row = jnp.where(lane == base, pairs_ref[0, 0, entry], row)
        row = jnp.where(lane == base + 1, pairs_ref[0, 1, entry], row)
        row = jnp.where(lane == base + 2, 1, row)
    return row


def correlate_kernel(
    groups, columns, phases, entries, windows, scale,
    pairs_hbm, owners_hbm, mask_hbm, strain_hbm, table_ref, inverse_ref, *rest,
):
    outs = 2 if phases > 1 else 1
    last_stack, total_hbm = rest[0], rest[outs - 1]
    pairs_ref, owners_ref, mask_ref, strain_ref, inverse_buf, left_buf = rest[outs : outs + 6]
    table_buf, white_buf, list_buf, lists_buf, lists_smem = rest[outs + 6 : outs + 11]
    total_ref, total_sem = rest[outs + 11 : outs + 13]
    rest = rest[outs + 13 :]
    rows_bufs, slot_bufs = rest[:phases], rest[phases : 2 * phases]
    stack_bufs = list(rest[2 * phases : 3 * phases - 1]) + [last_stack]
    in_sem, inverse_sem = rest[3 * phases - 1 : 3 * phases + 1]
    table_sem, own_sem, lsend_sem, lrecv_sem, wsend_sem, wrecv_sem, ssend_sem, srecv_sem = rest[
        3 * phases + 1 :
    ]
    devices = groups * columns
    my_group = lax.axis_index("grp")
    mine = lax.axis_index("ch")
    me = my_group * columns + mine
    tiles = phases * groups
    rows = white_buf.shape[2]
    half = rows // 2

    def tile_group(index):
        return lax.rem(index + my_group, groups)

    def tile_copy(index):
        place = lax.div(index, groups) * groups + tile_group(index)
        return pltpu.make_async_copy(
            table_ref.at[place], table_buf.at[index], table_sem.at[index]
        )

    inputs = [
        pltpu.make_async_copy(source, target, in_sem.at[place])
        for place, (source, target) in enumerate(
            [
                (pairs_hbm, pairs_ref),
                (owners_hbm, owners_ref),
                (mask_hbm, mask_ref),
                (strain_hbm, strain_ref),
            ]
        )
    ]
    for copy in inputs:
        copy.start()
    loop(0, tiles, lambda index: tile_copy(index).start())

    def inverse_copy(phase):
        return pltpu.make_async_copy(
            inverse_ref.at[phase], inverse_buf.at[phase], inverse_sem.at[phase]
        )

    for phase in range(phases - 1):
        inverse_copy(phase).start()

    barrier = pltpu.get_barrier_semaphore()

    def greet(step):
        to = lax.rem(me + step, devices)
        pl.semaphore_signal(
            barrier,
            inc=1,
            device_id=(lax.div(to, columns), lax.rem(to, columns)),
            device_id_type=MESH,
        )

    loop(1, devices, greet)
    for copy in inputs:
        copy.wait()
    list_buf[...] = slot_row(groups, entries, pairs_ref, owners_ref)

    def compute_tile(index):
        tile_copy(index).wait()
        spectrum = lax.dot_general(
            table_buf[index],
            strain_ref[...],
            (((1,), (1,)), ((), ())),
            preferred_element_type=jnp.float32,
        )
        lanes = spectrum.shape[1]
        parts = spectrum.reshape(columns, 2, half, lanes)
        power = parts[:, 0] * parts[:, 0] + parts[:, 1] * parts[:, 1]
        bands = columns * half // SUB
        band_power = jnp.sum(power.reshape(bands, SUB, lanes), axis=1, keepdims=True) / SUB
        usable = jnp.concatenate([mask_ref[w : w + 1, :] for w in range(windows)], axis=1)
        gain = usable.astype(jnp.float32).reshape(1, 1, lanes) / jnp.sqrt(band_power + 1e-06)
        gain = jnp.broadcast_to(gain, (bands, SUB, lanes)).reshape(columns, 1, half, lanes)
        white_buf[index] = (parts * gain).reshape(columns, rows, lanes).astype(jnp.bfloat16)

    def white_copy(phase, index, column):
        to_group = tile_group(index)
        to = to_group * columns + column
        return pltpu.make_async_remote_copy(
            src_ref=white_buf.at[index, column],
            dst_ref=rows_bufs[phase].at[me],
            send_sem=wsend_sem.at[phase, to],
            recv_sem=wrecv_sem.at[phase, me],
            device_id=(to_group, column),
            device_id_type=MESH,
        )

    def white_own(phase, index):
        return pltpu.make_async_copy(
            white_buf.at[index, mine], rows_bufs[phase].at[me], wrecv_sem.at[phase, me]
        )

    def send_tile(phase, index):
        def send(step):
            column = lax.rem(mine + step, columns)
            away = (tile_group(index) != my_group) | (column != mine)

            @pl.when(away)
            def _():
                white_copy(phase, index, column).start()

            @pl.when(jnp.logical_not(away))
            def _():
                white_own(phase, index).start()

        loop(0, columns, send)

    def list_copy(step):
        return pltpu.make_async_remote_copy(
            src_ref=list_buf,
            dst_ref=lists_buf.at[mine],
            send_sem=lsend_sem.at[step],
            recv_sem=lrecv_sem.at[step],
            device_id=(my_group, lax.rem(mine + step, columns)),
            device_id_type=MESH,
        )

    compute_tile(0)
    pl.semaphore_wait(barrier, devices - 1)
    loop(1, columns, lambda step: list_copy(step).start())
    own_list = pltpu.make_async_copy(list_buf, lists_buf.at[mine], own_sem.at[0])
    own_list.start()
    for phase in range(phases):

        def compute_and_send(index, phase=phase):
            compute_tile(index)
            send_tile(phase, index - 1)

        loop(phase * groups + 1, (phase + 1) * groups, compute_and_send)
        if phase + 1 < phases:
            compute_tile((phase + 1) * groups)
        send_tile(phase, (phase + 1) * groups - 1)

    own_list.wait()
    loop(1, columns, lambda step: list_copy(step).wait())
    to_smem = pltpu.make_async_copy(lists_buf, lists_smem, own_sem.at[1])
    to_smem.start()
    to_smem.wait()

    def slot_copy(phase, group, column):
        return pltpu.make_async_remote_copy(
            src_ref=slot_bufs[phase].at[group, column],
            dst_ref=stack_bufs[phase].at[:, me],
            send_sem=ssend_sem.at[phase, group * columns + column],
            recv_sem=srecv_sem.at[phase, me],
            device_id=(group, column),
            device_id_type=MESH,
        )

    def slot_own(phase):
        return pltpu.make_async_copy(
            slot_bufs[phase].at[my_group, mine], stack_bufs[phase].at[:, me], srecv_sem.at[phase, me]
        )

    def cross_column(phase, column):
        rows_ref = rows_bufs[phase]
        for owner in range(groups):
            for rank in range(CAP):
                base = 3 * (owner * CAP + rank)
                first = lists_smem[column, 0, base]
                second = lists_smem[column, 0, base + 1]
                factor = lists_smem[column, 0, base + 2].astype(jnp.float32) * scale
                real = jnp.zeros((half, BLK), jnp.float32)
                imag = jnp.zeros((half, BLK), jnp.float32)
                for group in range(groups):
                    a = rows_ref[group * columns + first].astype(jnp.float32)
                    b = rows_ref[group * columns + second].astype(jnp.float32)
                    for window in range(windows):
                        lanes = slice(window * BLK, (window + 1) * BLK)
                        a_real, a_imag = a[:half, lanes], a[half:, lanes]
                        b_real, b_imag = b[:half, lanes], b[half:, lanes]
                        real += a_real * b_real + a_imag * b_imag
                        imag += a_real * b_imag - a_imag * b_real
                both = jnp.concatenate([real, imag], axis=0) * factor
                slot_bufs[phase][owner, column, rank] = both.astype(jnp.bfloat16)

    def send_column(phase, column):
        def send(step):
            group = lax.rem(my_group + step, groups)
            away = (group != my_group) | (column != mine)

            @pl.when(away)
            def _():
                slot_copy(phase, group, column).start()

            @pl.when(jnp.logical_not(away))
            def _():
                slot_own(phase).start()

        loop(0, groups, send)

    def wait_from(phase, sem, part):
        def wait(source):
            @pl.when(source != me)
            def _():
                pltpu.make_async_remote_copy(
                    src_ref=part(source),
                    dst_ref=part(source),
                    send_sem=sem.at[phase, source],
                    recv_sem=sem.at[phase, source],
                    device_id=(lax.div(source, columns), lax.rem(source, columns)),
                    device_id_type=MESH,
                ).wait_recv()

        loop(0, devices, wait)

    for phase in range(phases):
        white_own(phase, phase * groups).wait()
        wait_from(phase, wrecv_sem, lambda source: rows_bufs[phase].at[source])

        cross_column(phase, mine)

        def cross_and_send(step, phase=phase):
            cross_column(phase, lax.rem(mine + step, columns))
            send_column(phase, lax.rem(mine + step - 1, columns))

        loop(1, columns, cross_and_send)
        send_column(phase, lax.rem(mine + columns - 1, columns))

    for phase in range(phases):
        slot_own(phase).wait()
        wait_from(phase, srecv_sem, lambda source: stack_bufs[phase].at[:, source])
        if phase < phases - 1:
            inverse_copy(phase).wait()
            depth = devices * rows
            for rank in range(CAP):
                block = stack_bufs[phase][rank].reshape(depth, BLK).astype(jnp.float32)
                left_buf[rank * BLK : (rank + 1) * BLK, :] = block.T.astype(jnp.bfloat16)

            def inverse_tile(tile, phase=phase):
                at = pl.ds(pl.multiple_of(tile * LAGS, LAGS), LAGS)
                part = jnp.dot(
                    left_buf[...], inverse_buf[phase, :, at], preferred_element_type=jnp.float32
                )
                total_ref[:, at] = part if phase == 0 else total_ref[:, at] + part

            loop(0, NFFT // LAGS, inverse_tile)
        if phase == phases - 2:
            total_copy = pltpu.make_async_copy(total_ref, total_hbm, total_sem.at[0])
            total_copy.start()


        def wait_sends(to, phase=phase):
            group, column = lax.div(to, columns), lax.rem(to, columns)

            @pl.when(to != me)
            def _():
                index = phase * groups + lax.rem(group - my_group + groups, groups)
                white_copy(phase, index, column).wait_send()
                slot_copy(phase, group, column).wait_send()

        loop(0, devices, wait_sends)
    if phases > 1:
        total_copy.wait()


def local(strain, valid_mask, pair_list, owner_group):
    windows, channels = valid_mask.shape
    groups = lax.axis_size("grp")
    columns = lax.axis_size("ch")
    devices = groups * columns
    entries = owner_group.shape[1]
    phases = phases_of(devices)
    rows = 2 * NB // devices // phases
    lanes = windows * channels
    tiles = phases * groups
    scale = 1.0 / math.sqrt(NB * windows * groups)

    vmem = pl.BlockSpec(memory_space=pltpu.VMEM)
    dma = pltpu.SemaphoreType.DMA
    anywhere = pl.BlockSpec(memory_space=pltpu.HBM)
    stack_shape = (CAP, devices, rows, BLK)
    depth = devices * rows
    outs = [jax.ShapeDtypeStruct(stack_shape, jnp.bfloat16)]
    if phases > 1:
        outs.append(jax.ShapeDtypeStruct((CAP * BLK, NFFT), jnp.float32))
    inverse = inverse_rows(devices).reshape(phases, depth, NFFT)
    stack, *total = pl.pallas_call(
        functools.partial(correlate_kernel, groups, columns, phases, entries, windows, scale),
        out_shape=outs,
        in_specs=[anywhere] * 6,
        out_specs=[vmem, anywhere][: len(outs)],
        scratch_shapes=[
            pltpu.SMEM((1, 2, entries), jnp.int32),
            pltpu.SMEM((1, entries), jnp.int32),
            pltpu.VMEM((windows, channels), jnp.int32),
            pltpu.VMEM((lanes, NFFT), jnp.bfloat16),
            pltpu.VMEM((max(1, phases - 1), depth if phases > 1 else 16, NFFT), jnp.bfloat16),
            pltpu.VMEM((CAP * BLK, depth), jnp.bfloat16),
            pltpu.VMEM((tiles, columns * rows, NFFT), jnp.bfloat16),
            pltpu.VMEM((tiles, columns, rows, lanes), jnp.bfloat16),
            pltpu.VMEM((8, LANES), jnp.int32),
            pltpu.VMEM((columns, 8, LANES), jnp.int32),
            pltpu.SMEM((columns, 8, LANES), jnp.int32),
            pltpu.VMEM((CAP * BLK, NFFT if phases > 1 else LANES), jnp.float32),
            dma((1,)),
        ]
        + [pltpu.VMEM((devices, rows, lanes), jnp.bfloat16) for _ in range(phases)]
        + [pltpu.VMEM((groups, columns, CAP, rows, BLK), jnp.bfloat16) for _ in range(phases)]
        + [pltpu.VMEM(stack_shape, jnp.bfloat16) for _ in range(phases - 1)]
        + [dma((4,)), dma((phases,))]
        + [dma((tiles,)), dma((2,)), dma((columns,)), dma((columns,))]
        + [dma((phases, devices)) for _ in range(4)],
        compiler_params=pltpu.CompilerParams(
            collective_id=0, has_side_effects=True, vmem_limit_bytes=52 * 1024 * 1024
        ),
    )(
        pair_list.transpose(0, 2, 1),
        owner_group,
        valid_mask,
        strain.reshape(lanes, NFFT),
        jnp.asarray(forward_rows(devices)).reshape(tiles, columns * rows, NFFT),
        jnp.asarray(inverse[: max(1, phases - 1)]),
    )
    stacked = jnp.einsum(
        "skr,kt->srt",
        stack.reshape(CAP, depth, BLK),
        jnp.asarray(inverse[phases - 1]),
        preferred_element_type=jnp.float32,
    )
    if phases > 1:
        stacked = stacked + total[0].reshape(CAP, BLK, NFFT)
    return stacked.reshape(1, 1, CAP, BLK, NFFT)


def solution(mesh):
    placed = (P("grp", "ch", None), P("grp", "ch"), P("ch", None, None), P("ch", None))
    return jax.shard_map(
        local,
        mesh=mesh,
        in_specs=placed,
        out_specs=P("grp", "ch", None, None, None),
        check_vma=False,
    )
```
